256 devices in a mesh: wide: 32 (over x, z), narrow: 8 (over y, core).
Axes of the slice: x: 4, y: 4, z: 8, core: 2. Of those that a mesh axis runs over, the one named last changes fastest.
Arguments:
- patches: bfloat16 [3200, 32768], P('wide', 'narrow')
- ln_gain: bfloat16 [4, 3200], P(None, 'wide'), may hold values from 0.5 to 1.5
- ln_bias: bfloat16 [4, 3200], P(None, 'wide'), may hold values from -3 to 3
- first_weight: bfloat16 [4, 3200, 6144], P(None, 'wide', 'narrow'), may hold values from -0.0546875 to 0.0546875
- first_bias: bfloat16 [6144], P('narrow'), may hold values from -3 to 3
- second_weight: bfloat16 [6144, 6144], P('wide', 'narrow'), may hold values from -0.078125 to 0.078125
- second_bias: bfloat16 [6144], P('wide'), may hold values from -3 to 3
- text_embeds: bfloat16 [6144, 10240], P('wide', 'narrow'), may hold values from -6 to 6
- vis_pos: int32 [8192], replicated, may hold values from 0 to 10239, as said below
Outputs:
- prompt_embeds: bfloat16 [6144, 10240], P('wide', 'narrow')
The draws below stay inside these ranges and needn't reach their ends.
Inputs may be any that keep to these rules, and one draw needn't show every extreme that they name: vis_pos is strictly increasing and made of runs of 256 consecutive prompt rows, one run per tile in tile order; the first visual row is the first prompt row and the last visual row is the last prompt row.
All inputs are finite; a program needn't handle non-finite values.
Results may differ from the reference program's by a relative error of at most 0.012.
Values may be sent and summed in bfloat16 or wider, within the bound.
A program may use at most 128 MiB of HBM per device.

```python
import math
import jax
import jax.numpy as jnp
from jax import lax

D = 3200
E = 6144
TILE_SIDE = 32
TILE_ROWS = 256
TILES = 32
T_ROWS = 32768
VIS = 8192
TEXT = 2048
PROMPT = 10240


def draw_patches(key, part):
    first_key, second_key, third_key = jax.random.split(jax.random.fold_in(key, 11), 3)
    position = jnp.arange(D, dtype=jnp.float32) / D
    spread = jnp.exp(jax.random.uniform(second_key, (D,), jnp.float32, 0.0, math.log(10.0 / 3.0)))
    column = jnp.exp(position * math.log(3.0)) * spread
    base = jax.random.normal(first_key, (T_ROWS, D), jnp.float32)
    row_scale = jnp.exp(jax.random.uniform(third_key, (T_ROWS,), jnp.float32, 0.0, math.log(10.0)))
    return (base * row_scale[:, None] * column[None, :]).T.astype(jnp.bfloat16)


def draw_vis_pos(key, part):
    cut_key = jax.random.fold_in(key, 23)
    cuts = jax.random.randint(cut_key, (TILES,), 0, TEXT + 1)
    cuts = jnp.sort(cuts)
    cuts = cuts.at[0].set(0)
    cuts = cuts.at[TILES - 1].set(TEXT)
    starts = cuts + jnp.arange(TILES, dtype=jnp.int32) * TILE_ROWS
    offsets = jnp.arange(TILE_ROWS, dtype=jnp.int32)
    return (starts[:, None] + offsets[None, :]).reshape(VIS).astype(jnp.int32)


def block_scale(stream_key, dims, cuts, low, largest):
    def one(axis_at, shards_of):
        steps = jax.random.uniform(jax.random.fold_in(jax.random.fold_in(stream_key, 6), axis_at), (shards_of,), jnp.float32, low / len(cuts), largest / len(cuts))
        return jnp.repeat(jnp.exp(steps), dims[axis_at] // shards_of).reshape((-1,) + (1,) * (len(dims) - axis_at - 1))

    factor_of = one(*cuts[0])
    for cut in cuts[1:]:
        factor_of = factor_of * one(*cut)
    return factor_of


def centred(stream_key, dims, width, reach, cuts=(), kind=jnp.bfloat16):
    array = width * jax.random.normal(stream_key, dims, jnp.float32)
    if cuts:
        array = array * block_scale(stream_key, dims, cuts, -0.22, 0.18)
    return jnp.clip(array, -reach, reach).astype(kind)


def setup_inputs(seed: int = 0) -> dict:
    splits = jax.random.split(jax.random.key(seed), 10)
    patches = draw_patches(jax.random.fold_in(splits[9], 71), 0)
    ln_gain = jnp.clip(0.5 + 1.0 * jax.random.uniform(splits[1], (4, D), jnp.float32) ** block_scale(splits[1], (4, D), ((1, 32),), -0.2, 0.2), 0.5, 1.5).astype(jnp.bfloat16)
    ln_bias = centred(splits[2], (4, D), 0.5, 3.0, ((1, 32),))
    first_weight = centred(splits[3], (4, D, E), (4 * D) ** -0.5, 0.0546875, ((1, 32), (2, 8)))
    first_bias = centred(splits[4], (E,), 0.5, 3.0, ((0, 8),))
    second_weight = centred(splits[5], (E, E), E ** -0.5, 0.078125, ((0, 32), (1, 8)))
    second_bias = centred(splits[6], (E,), 0.5, 3.0, ((0, 32),))
    text_embeds = centred(splits[7], (E, PROMPT), 1.0, 6.0, ((0, 32), (1, 8)))
    vis_pos = draw_vis_pos(jax.random.fold_in(splits[9], 71), 0)
    return {"patches": patches, "ln_gain": ln_gain, "ln_bias": ln_bias, "first_weight": first_weight, "first_bias": first_bias, "second_weight": second_weight, "second_bias": second_bias, "text_embeds": text_embeds, "vis_pos": vis_pos}


def reference(patches, ln_gain, ln_bias, first_weight, first_bias, second_weight, second_bias, text_embeds, vis_pos):
    half_side = TILE_SIDE // 2
    patch_rows = patches.T
    merged = patch_rows.reshape(TILES, half_side, 2, half_side, 2, D).transpose(0, 1, 3, 2, 4, 5).reshape(VIS, 4, D)
    float_rows = merged.astype(jnp.float32)
    entries = 4.0 * D
    row_mean = lax.optimization_barrier(jnp.sum(float_rows, axis=(1, 2))) / entries
    row_var = lax.optimization_barrier(jnp.sum(float_rows * float_rows, axis=(1, 2))) / entries - row_mean * row_mean
    inverse = lax.rsqrt(row_var + 1e-05)
    normed = ((float_rows - row_mean[:, None, None]) * inverse[:, None, None] * ln_gain.astype(jnp.float32) + ln_bias.astype(jnp.float32)).astype(jnp.bfloat16)
    preact = jnp.dot(normed.reshape(VIS, 4 * D), first_weight.reshape(4 * D, E), preferred_element_type=jnp.float32)
    preact = preact + first_bias.astype(jnp.float32)
    activated = jax.nn.gelu(preact, approximate=False).astype(jnp.bfloat16)
    visual = jnp.dot(second_weight, activated.T, preferred_element_type=jnp.float32) + second_bias.astype(jnp.float32)[:, None]
    visual = visual.astype(jnp.bfloat16)
    return text_embeds.at[:, vis_pos.astype(jnp.int32)].set(visual)
```

```python
import functools

import jax
import jax.numpy as jnp
from jax import lax
from jax.experimental import pallas as pl
from jax.experimental.pallas import tpu as pltpu
from jax.sharding import PartitionSpec as P

MESH = pl.DeviceIdType.MESH
F32 = jnp.float32
BF16 = jnp.bfloat16
NX, NZ, NY = 4, 8, 4
TILE_SIDE = 32
TILE_ROWS = 256
SLOTS = 13


def rem(a, m):
    return lax.rem(a, m)


def wait(ref, sem):
    pltpu.make_async_copy(ref, ref, sem).wait()


def send(src, dst, send_sem, recv_sem, **where):
    pltpu.make_async_remote_copy(
        src_ref=src,
        dst_ref=dst,
        send_sem=send_sem,
        recv_sem=recv_sem,
        device_id=where,
        device_id_type=MESH,
    ).start()


class Mover:
    def __init__(self, at, src, wy, wg, ra, rb, yr, wr, pr, rr, ys, xs, ps, rs, ls):
        self.at, self.src, self.wy, self.wg, self.relay_bufs = at, src, wy, wg, (ra, rb)
        self.yr, self.wr, self.pr, self.rr = yr, wr, pr, rr
        self.ys, self.xs, self.ps, self.rs, self.ls = ys, xs, ps, rs, ls
        self.width = src.shape[1]
        self.half = self.width // 2

    def hs(self, h):
        return pl.ds(h * self.half, self.half)

    def cols(self, core, h):
        return pl.ds(pl.multiple_of(core * self.width + h * self.half, 128), self.half)

    def load(self):
        copy = pltpu.make_async_copy(self.src, self.wy.at[self.at["y"]], self.ls)
        copy.start()
        copy.wait()

    def ysend(self, i, slot, h, up):
        at = self.at
        n = rem(at["n"] + (2 if up else 2 * NY - 2), 2 * NY)
        ref = self.wy.at[slot, :, self.hs(h)]
        send(ref, ref, self.ys.at[i], self.yr.at[slot, h], narrow=n)

    def start_y(self):
        y = self.at["y"]
        self.ysend(0, y, 0, True)
        self.ysend(1, y, 1, False)
        self.ysend(2, y, 1, True)
        self.ysend(3, y, 0, False)

    def yslot(self, dy):
        return rem(self.at["y"] + dy + NY, NY)

    def wait_y(self, dy, h):
        slot = self.yslot(dy)
        wait(self.wy.at[slot, :, self.hs(h)], self.yr.at[slot, h])

    def fwd_y(self):
        self.wait_y(-1, 0)
        self.ysend(4, self.yslot(-1), 0, True)
        self.wait_y(1, 1)
        self.ysend(5, self.yslot(1), 1, False)

    def xf(self, dy, h):
        at = self.at
        x, z, c = at["x"], at["z"], at["c"]
        i = (dy + NY) % NY
        ysrc = self.yslot(dy)
        d = rem(ysrc - x + NX, NX)
        src = self.wy.at[ysrc, :, self.hs(h)]
        dst = self.wg.at[x, :, self.cols(c, h)]
        step = 1 if h == 0 else NX - 1

        @pl.when(d == 0)
        def _():
            pltpu.make_async_copy(src, dst, self.wr.at[x, h]).start()

        @pl.when(rem(d, 2) == 1)
        def _():
            send(src, dst, self.xs.at[i, h], self.wr.at[x, h], wide=ysrc * NZ + z)

        @pl.when(d == 2)
        def _():
            send(src, self.relay_bufs[h], self.xs.at[i, h], self.rr.at[h], wide=rem(x + step, NX) * NZ + z)

    def relay(self, h):
        at = self.at
        x, z, c = at["x"], at["z"], at["c"]
        step = 1 if h == 0 else NX - 1
        k = rem(x + NX - step, NX)
        buf = self.relay_bufs[h]
        wait(buf, self.rr.at[h])
        send(buf, self.wg.at[k, :, self.cols(c, h)], self.rs.at[h], self.wr.at[k, h], wide=rem(x + step, NX) * NZ + z)

    def cex(self, dk, h):
        at = self.at
        k = rem(at["x"] + dk + NX, NX)
        ref = self.wg.at[k, :, self.cols(at["c"], h)]
        wait(ref, self.wr.at[k, h])
        send(ref, ref, self.ps.at[k, h], self.pr.at[k, h], narrow=2 * at["y"] + 1 - at["c"])

    def finish(self):
        for k in range(NX):
            for h in range(2):
                wait(self.wg.at[k, :, self.cols(1 - self.at["c"], h)], self.pr.at[k, h])

    def wait_sends(self):
        at = self.at
        ref = self.wy.at[0, :, self.hs(0)]
        for i in range(6):
            wait(ref, self.ys.at[i])
        for i in range(NY):
            d = rem(self.yslot(i) - at["x"] + NX, NX)
            for h in range(2):

                @pl.when(d != 0)
                def _():
                    wait(ref, self.xs.at[i, h])

        for h in range(2):
            wait(ref, self.rs.at[h])
        for k in range(NX):
            for h in range(2):
                wait(ref, self.ps.at[k, h])


def mover_scratch(rows, width):
    dma = pltpu.SemaphoreType.DMA
    return [
        pltpu.VMEM((NY, rows, width), BF16),
        pltpu.VMEM((NX, rows, 2 * width), BF16),
        pltpu.VMEM((rows, width // 2), BF16),
        pltpu.VMEM((rows, width // 2), BF16),
        dma((NY, 2)),
        dma((NX, 2)),
        dma((NX, 2)),
        dma((2,)),
        dma((6,)),
        dma((NY, 2)),
        dma((NX, 2)),
        dma((2,)),
        dma(()),
    ]


def project(entries, w1_ref, w2_ref, p_ref, gb_ref, b2_ref, v_ref, *scratch):
    m1s, m2s, rest = scratch[:13], scratch[13:26], scratch[26:]
    (xf, sx, sz, sxr, sxs, szr, szs, xg, xgr, xgs, xt, part, rz, rzr, rzs, act, ar, asend_sem, ob, orx, orr, ors, vst, vr, vsend) = rest
    wide, n = lax.axis_index("wide"), lax.axis_index("narrow")
    x, z = wide // NZ, rem(wide, NZ)
    y, c = n // 2, rem(n, 2)
    at = {"x": x, "y": y, "z": z, "c": c, "n": n}
    feats = p_ref.shape[0]
    krows = 4 * feats
    rows = xg.shape[2]
    hid = m1s[1].shape[2]
    outs = w2_ref.shape[0]
    block = rows // NZ

    def xdev(d):
        return rem(x + d, NX) * NZ + z

    def zdev(d):
        return x * NZ + rem(z + d, NZ)

    barrier = pltpu.get_barrier_semaphore()
    for d in range(1, NX):
        pl.semaphore_signal(barrier, inc=1, device_id={"wide": xdev(d)}, device_id_type=MESH)
    for d in range(1, NZ):
        pl.semaphore_signal(barrier, inc=1, device_id={"wide": zdev(d)}, device_id_type=MESH)
    for d in (1, 2, 2 * NY - 2, 2 * NY - 1):
        pl.semaphore_signal(barrier, inc=1, device_id={"narrow": rem(n + d, 2 * NY)}, device_id_type=MESH)
    pl.semaphore_wait(barrier, NX - 1 + NZ - 1 + 4)

    first = Mover(at, w1_ref, *m1s)
    second = Mover(at, w2_ref, *m2s)
    first.load()
    first.start_y()
    for h in range(2):
        first.xf(0, h)
    second.load()

    lane = lax.broadcasted_iota(jnp.int32, (512, 512), 0)
    goal = (lane // 32 % 2 * 2 + lane % 2) * 128 + lane // 64 * 16 + lane % 32 // 2
    perm = jnp.where(goal == lax.broadcasted_iota(jnp.int32, (512, 512), 1), 1.0, 0.0).astype(BF16)
    for g in range(p_ref.shape[1] // 512):
        moved = jnp.dot(p_ref[:, g * 512 : (g + 1) * 512], perm, preferred_element_type=F32)
        for s in range(4):
            xf[s * feats : (s + 1) * feats, g * 128 : (g + 1) * 128] = moved[:, s * 128 : (s + 1) * 128]

    def gather_sums(i, carry):
        v = xf[pl.ds(pl.multiple_of(i * 8, 8), 8), :]
        return carry[0] + v, carry[1] + v * v

    zero = jnp.zeros((8, rows), F32)
    sums = lax.fori_loop(0, krows // 8, gather_sums, (zero, zero))
    sx[x, 0:1, :] = jnp.sum(sums[0], axis=0, keepdims=True)
    sx[x, 1:2, :] = jnp.sum(sums[1], axis=0, keepdims=True)
    for d in range(1, NX):
        send(sx.at[x], sx.at[x], sxs.at[d], sxr.at[x], wide=xdev(d))
    for d in range(1, NX):
        k = rem(x + d, NX)
        wait(sx.at[k], sxr.at[k])
    sz[z] = (sx[0] + sx[1]) + (sx[2] + sx[3])
    for d in range(1, NZ):
        send(sz.at[z], sz.at[z], szs.at[d], szr.at[z], wide=zdev(d))
    for d in range(1, NZ):
        k = rem(z + d, NZ)
        wait(sz.at[k], szr.at[k])
    total = sz[0]
    for k in range(1, NZ):
        total = total + sz[k]
    mean = total[0:1, :] / entries
    inverse = lax.rsqrt(total[1:2, :] / entries - mean * mean + 1e-05)

    def normalise(i, carry):
        at_rows = pl.ds(pl.multiple_of(i * 16, 16), 16)
        gain_shift = gb_ref[at_rows, :]
        v = (xf[at_rows, :] - mean) * inverse * gain_shift[:, 0:1] + gain_shift[:, 1:2]
        xg[x, at_rows, :] = v.astype(BF16)
        return carry

    lax.fori_loop(0, krows // 16, normalise, 0)

    def xsend(i, k, h, d):
        ref = xg.at[k, :, pl.ds(h * (rows // 2), rows // 2)]
        send(ref, ref, xgs.at[i], xgr.at[k, h], wide=xdev(d))

    def xwait(d, h):
        k = rem(x + d, NX)
        wait(xg.at[k, :, pl.ds(h * (rows // 2), rows // 2)], xgr.at[k, h])

    first.fwd_y()
    xsend(0, x, 0, 1)
    xsend(1, x, 1, NX - 1)
    xsend(2, x, 1, 1)
    xsend(3, x, 0, NX - 1)
    first.xf(-1, 0)
    first.xf(1, 1)
    first.wait_y(-1, 1)
    first.xf(-1, 1)
    first.wait_y(1, 0)
    first.xf(1, 0)
    second.start_y()
    xwait(NX - 1, 0)
    xsend(4, rem(x + NX - 1, NX), 0, 1)
    xwait(1, 1)
    xsend(5, rem(x + 1, NX), 1, NX - 1)
    first.wait_y(2, 0)
    first.xf(2, 0)
    first.wait_y(2, 1)
    first.xf(2, 1)
    first.relay(0)
    first.relay(1)
    second.fwd_y()
    for h in range(2):
        second.xf(0, h)
        first.cex(0, h)
    first.cex(-1, 0)
    first.cex(1, 1)
    first.cex(-1, 1)
    first.cex(1, 0)
    first.cex(2, 0)
    first.cex(2, 1)
    xwait(NX - 1, 1)
    xwait(1, 0)
    xwait(2, 0)
    xwait(2, 1)
    first.finish()

    w1g, w2g = m1s[1], m2s[1]
    chunk = hid // 4
    rz[0] = jnp.zeros(rz.shape[1:], BF16)

    def block_of(b):
        return pl.ds(pl.multiple_of(b * block, block), block)

    def multiply(s):
        ba = rem(z - 1 - s + NZ, NZ)
        bb = jnp.where(s == NZ // 2 - 1, z, rem(z + 1 + s, NZ))
        for k in range(NX):
            pair = jnp.concatenate([xg[k, :, block_of(ba)], xg[k, :, block_of(bb)]], axis=1)
            xt[:, k * krows : (k + 1) * krows] = pair.T
        left = xt[...]

        def tile(j, carry):
            at_cols = pl.ds(pl.multiple_of(j * 512, 512), 512)
            right = w1g[:, 0:krows, at_cols].reshape(NX * krows, 512)
            out = jnp.dot(left, right, preferred_element_type=F32)
            part[ba, :, at_cols] = out[:block]
            part[bb, :, at_cols] = out[block:]
            return carry

        lax.fori_loop(0, hid // 512, tile, 0)

    def reduce_step(s):
        for f in (0, 2, 1, 3):
            up = f < 2
            b = rem(z - 1 - s + NZ, NZ) if up else rem(z + 1 + s, NZ)

            @pl.when(s > 0)
            def _():
                wait(rz.at[s, f], rzr.at[s, f])

            own = part[b, :, f * chunk : (f + 1) * chunk]
            rz[s, f] = (rz[s, f].astype(F32) + own).astype(BF16)
            send(rz.at[s, f], rz.at[s + 1, f], rzs.at[s, f], rzr.at[s + 1, f], wide=zdev(1 if up else NZ - 1))

    def front(s, carry):
        multiply(s)
        reduce_step(s)
        return carry

    lax.fori_loop(0, NZ // 2, front, 0)
    second.xf(-1, 0)
    second.xf(1, 1)
    second.wait_y(-1, 1)
    second.xf(-1, 1)
    second.wait_y(1, 0)
    second.xf(1, 0)
    for h in range(2):
        second.wait_y(2, h)
        second.xf(2, h)

    def back(s, carry):
        reduce_step(s)
        return carry

    lax.fori_loop(NZ // 2, NZ - 1, back, 0)
    second.relay(0)
    second.relay(1)

    half_root = 0.7071067811865476
    for f in (0, 2, 1, 3):
        at_cols = slice(f * chunk, (f + 1) * chunk)
        wait(rz.at[NZ - 1, f], rzr.at[NZ - 1, f])
        shift = w1g[0, krows : krows + 16, at_cols].astype(F32)[0:1, :]
        v = rz[NZ - 1, f].astype(F32) + part[z, :, at_cols] + shift
        act[z, :, at_cols] = (0.5 * v * (1.0 + lax.erf(v * half_root))).astype(BF16)

    half = hid // 2

    def asend(s, b, h, up):
        ref = act.at[b, :, pl.ds(h * half, half)]
        send(ref, ref, asend_sem.at[0 if up else 1, s, h], ar.at[b, h], wide=zdev(1 if up else NZ - 1))

    def await_act(b, h):
        wait(act.at[b, :, pl.ds(h * half, half)], ar.at[b, h])

    for h, up in ((0, True), (1, False), (1, True), (0, False)):
        asend(0, z, h, up)
    for h in range(2):
        second.cex(0, h)
    for dk, h in ((-1, 0), (1, 1), (-1, 1), (1, 0), (2, 0), (2, 1)):
        second.cex(dk, h)
    second.finish()

    def blocks_at(s):
        return rem(z - s + NZ, NZ), jnp.where(s == NZ // 2, z, rem(z + s, NZ))

    def gather_step(s):
        ba, bb = blocks_at(s)
        more = s < NZ // 2
        await_act(ba, 0)

        @pl.when(more)
        def _():
            asend(s, ba, 0, True)
            await_act(bb, 1)
            asend(s, bb, 1, False)

        await_act(ba, 1)

        @pl.when(s < NZ // 2 - 1)
        def _():
            asend(s, ba, 1, True)

        @pl.when(more)
        def _():
            await_act(bb, 0)

        @pl.when(s < NZ // 2 - 1)
        def _():
            asend(s, bb, 0, False)

        left = jnp.concatenate([act[ba], act[bb]], axis=0)

        def out_block(k, carry):
            out = lax.dot_general(w2g[k], left, (((1,), (1,)), ((), ())), preferred_element_type=F32)
            ob[s - 1, k] = out.astype(BF16)
            return carry

        lax.fori_loop(0, NX, out_block, 0)
        for d in range(1, NX):
            k = rem(x + d, NX)
            send(ob.at[s - 1, k], orx.at[s - 1, x], ors.at[s - 1, d], orr.at[s - 1, x], wide=xdev(d))

    def outgoing(d, t):
        q = n + d
        slot = t - 5 * q + 8
        ok = (q >= 0) & (q < 2 * NY) & (slot >= 0) & (slot < SLOTS)
        return q, slot, ok

    def finish_step(s):
        for d in range(1, NX):
            k = rem(x + d, NX)
            wait(orx.at[s - 1, k], orr.at[s - 1, k])
        value = ob[s - 1, x].astype(F32) + b2_ref[...]
        for d in range(1, NX):
            value = value + orx[s - 1, rem(x + d, NX)].astype(F32)
        value = value.astype(BF16)
        for i, b in enumerate(blocks_at(s)):
            vst[s - 1, i] = value[:, i * block : (i + 1) * block]
            src = vst.at[s - 1, i]
            t = 4 * n + b // 2
            own = 2 * (t - 5 * n + 8) + rem(b, 2)
            pltpu.make_async_copy(src, v_ref.at[own], vr.at[own]).start()
            for j, d in enumerate((-2, -1, 1, 2)):
                q, slot, ok = outgoing(d, t)

                @pl.when(ok)
                def _():
                    there = 2 * slot + rem(b, 2)
                    send(src, v_ref.at[there], vsend.at[s - 1, i, j], vr.at[there], narrow=q)

    def last(s, carry):
        gather_step(s)

        @pl.when(s > 1)
        def _():
            finish_step(s - 1)

        return carry

    lax.fori_loop(1, NZ // 2 + 1, last, 0)
    finish_step(NZ // 2)

    for there in range(2 * SLOTS):
        t = 5 * n - 8 + there // 2

        @pl.when((t >= 0) & (t < 8 * NY))
        def _():
            wait(vst.at[0, 0], vr.at[there])

    for s in range(1, NZ // 2 + 1):
        for i, b in enumerate(blocks_at(s)):
            t = 4 * n + b // 2
            for j, d in enumerate((-2, -1, 1, 2)):
                ok = outgoing(d, t)[2]

                @pl.when(ok)
                def _():
                    wait(vst.at[0, 0], vsend.at[s - 1, i, j])

        for d in range(1, NX):
            wait(ob.at[0, 0], ors.at[s - 1, d])
    for s in range(NZ // 2):
        for h in range(2):
            for up in range(2):
                if s < NZ // 2 - 1 or h == up:
                    wait(act.at[0, :, pl.ds(0, half)], asend_sem.at[up, s, h])
    for s in range(NZ - 1):
        for f in range(4):
            wait(rz.at[0, 0], rzs.at[s, f])
    for d in range(1, NX):
        wait(sx.at[0], sxs.at[d])
    for d in range(1, NZ):
        wait(sz.at[0], szs.at[d])
    for i in range(6):
        wait(xg.at[0, :, pl.ds(0, rows // 2)], xgs.at[i])
    first.wait_sends()
    second.wait_sends()


def place(pos_ref, v_ref, text_ref, out_ref, acc, covered):
    n = lax.axis_index("narrow")
    cols = text_ref.shape[1]
    acc[...] = jnp.zeros_like(acc)
    covered[...] = jnp.zeros_like(covered)

    def step(slot, carry):
        t = 5 * n - 8 + slot
        valid = (t >= 0) & (t < 8 * NY)
        start = pos_ref[jnp.clip(t, 0, 8 * NY - 1) * TILE_ROWS] - n * cols

        @pl.when(valid & (start > -TILE_ROWS) & (start < cols))
        def _():
            row = lax.broadcasted_iota(jnp.int32, (TILE_ROWS, cols), 0)
            col = lax.broadcasted_iota(jnp.int32, (TILE_ROWS, cols), 1)
            hot = jnp.where(row + start == col, 1.0, 0.0).astype(BF16)
            tile = jnp.concatenate([v_ref[2 * slot], v_ref[2 * slot + 1]], axis=1)
            acc[...] += jnp.dot(tile, hot, preferred_element_type=F32)
            at_col = lax.broadcasted_iota(jnp.int32, covered.shape, 1)
            inside = (at_col >= start) & (at_col < start + TILE_ROWS)
            covered[...] = jnp.where(inside, 1.0, covered[...])

        return carry

    lax.fori_loop(0, SLOTS, step, 0)
    out_ref[...] = jnp.where(covered[0:1, :] > 0, acc[...].astype(BF16), text_ref[...])


def shards(patches, ln_gain, ln_bias, first_weight, first_bias, second_weight, second_bias, text_embeds, vis_pos):
    feats = patches.shape[0]
    krows = 4 * feats
    rows = patches.shape[1] // 4
    width = first_weight.shape[2]
    hid = 2 * width
    outs = second_weight.shape[0]
    block = rows // NZ
    w1 = jnp.concatenate(
        [first_weight.reshape(krows, width), first_bias[None, :], jnp.zeros((15, width), BF16)], axis=0
    )
    gb = jnp.stack([ln_gain.reshape(krows), ln_bias.reshape(krows)], axis=1).astype(F32)
    b2 = second_bias.astype(F32)[:, None]
    dma = pltpu.SemaphoreType.DMA
    vmem = pl.BlockSpec(memory_space=pltpu.VMEM)
    scratch = (
        mover_scratch(krows + 16, width)
        + mover_scratch(outs, width)
        + [
            pltpu.VMEM((krows, rows), F32),
            pltpu.VMEM((NX, 2, rows), F32),
            pltpu.VMEM((NZ, 2, rows), F32),
            dma((NX,)),
            dma((NX,)),
            dma((NZ,)),
            dma((NZ,)),
            pltpu.VMEM((NX, krows, rows), BF16),
            dma((NX, 2)),
            dma((6,)),
            pltpu.VMEM((2 * block, NX * krows), BF16),
            pltpu.VMEM((NZ, block, hid), F32),
            pltpu.VMEM((NZ, 4, block, hid // 4), BF16),
            dma((NZ, 4)),
            dma((NZ, 4)),
            pltpu.VMEM((NZ, block, hid), BF16),
            dma((NZ, 2)),
            dma((2, NZ // 2, 2)),
            pltpu.VMEM((NZ // 2, NX, outs, 2 * block), BF16),
            pltpu.VMEM((NZ // 2, NX, outs, 2 * block), BF16),
            dma((NZ // 2, NX)),
            dma((NZ // 2, NX)),
            pltpu.VMEM((NZ // 2, 2, outs, block), BF16),
            dma((2 * SLOTS,)),
            dma((NZ // 2, 2, 4)),
        ]
    )
    moved = pl.pallas_call(
        functools.partial(project, float(4 * feats * NX * NZ)),
        out_shape=jax.ShapeDtypeStruct((2 * SLOTS, outs, block), BF16),
        in_specs=[vmem] * 5,
        out_specs=pl.BlockSpec(memory_space=pl.ANY),
        scratch_shapes=scratch,
        compiler_params=pltpu.CompilerParams(
            collective_id=0, has_side_effects=True, vmem_limit_bytes=62 * 1024 * 1024
        ),
        name="project",
    )(w1, second_weight, patches, gb, b2)
    return pl.pallas_call(
        place,
        out_shape=jax.ShapeDtypeStruct(text_embeds.shape, BF16),
        in_specs=[pl.BlockSpec(memory_space=pltpu.SMEM), vmem, vmem],
        out_specs=vmem,
        scratch_shapes=[pltpu.VMEM(text_embeds.shape, F32), pltpu.VMEM((8, text_embeds.shape[1]), F32)],
        name="place",
    )(vis_pos, moved, text_embeds)


def solution(mesh):
    in_specs = (
        P("wide", "narrow"),
        P(None, "wide"),
        P(None, "wide"),
        P(None, "wide", "narrow"),
        P("narrow"),
        P("wide", "narrow"),
        P("wide"),
        P("wide", "narrow"),
        P(),
    )
    out_specs = P("wide", "narrow")
    return jax.shard_map(shards, mesh=mesh, in_specs=in_specs, out_specs=out_specs, check_vma=False)
```

```python
import functools

import jax
import jax.numpy as jnp
from jax import lax
from jax.experimental import pallas as pl
from jax.experimental.pallas import tpu as pltpu
from jax.sharding import PartitionSpec as P

MESH = pl.DeviceIdType.MESH
F32 = jnp.float32
BF16 = jnp.bfloat16
NX, NZ, NY = 4, 8, 4
TILE_SIDE = 32
TILE_ROWS = 256
SLOTS = 13


def rem(a, m):
    return lax.rem(a, m)


def wait(ref, sem):
    pltpu.make_async_copy(ref, ref, sem).wait()


def send(src, dst, send_sem, recv_sem, **where):
    pltpu.make_async_remote_copy(
        src_ref=src,
        dst_ref=dst,
        send_sem=send_sem,
        recv_sem=recv_sem,
        device_id=where,
        device_id_type=MESH,
    ).start()


class Mover:
    def __init__(self, at, wy, wg, ra, rb, yr, wr, pr, rr, ys, xs, ps, rs, ls):
        self.at, self.wy, self.wg, self.relay_bufs = at, wy, wg, (ra, rb)
        self.yr, self.wr, self.pr, self.rr = yr, wr, pr, rr
        self.ys, self.xs, self.ps, self.rs, self.ls = ys, xs, ps, rs, ls
        self.half = wy.shape[1] // 2
        self.width = wy.shape[2]

    def hs(self, h):
        return pl.ds(h * self.half, self.half)

    def spot(self, k, core, h):
        cols = pl.ds(pl.multiple_of(core * self.width, 128), self.width)
        return self.wg.at[k, self.hs(h), cols]

    def load(self, parts):
        copies = []
        for i, (src, row, count) in enumerate(parts):
            copies.append(pltpu.make_async_copy(src, self.wy.at[self.at["y"], pl.ds(row, count), :], self.ls.at[i]))
        for copy in copies:
            copy.start()
        for copy in copies:
            copy.wait()

    def ysend(self, i, slot, h, up):
        n = rem(self.at["n"] + (2 if up else 2 * NY - 2), 2 * NY)
        ref = self.wy.at[slot, self.hs(h), :]
        send(ref, ref, self.ys.at[i], self.yr.at[slot, h], narrow=n)

    def start_y(self):
        y = self.at["y"]
        self.ysend(0, y, 0, True)
        self.ysend(1, y, 1, False)
        self.ysend(2, y, 1, True)
        self.ysend(3, y, 0, False)

    def yslot(self, dy):
        return rem(self.at["y"] + dy + NY, NY)

    def wait_y(self, dy, h):
        slot = self.yslot(dy)
        wait(self.wy.at[slot, self.hs(h), :], self.yr.at[slot, h])

    def fwd_y(self):
        self.wait_y(-1, 0)
        self.ysend(4, self.yslot(-1), 0, True)
        self.wait_y(1, 1)
        self.ysend(5, self.yslot(1), 1, False)

    def xf(self, dy, h):
        at = self.at
        x, z, c = at["x"], at["z"], at["c"]
        i = (dy + NY) % NY
        ysrc = self.yslot(dy)
        d = rem(ysrc - x + NX, NX)
        src = self.wy.at[ysrc, self.hs(h), :]
        dst = self.spot(x, c, h)
        step = 1 if h == 0 else NX - 1

        @pl.when(d == 0)
        def _():
            pltpu.make_async_copy(src, dst, self.wr.at[x, h]).start()

        @pl.when(rem(d, 2) == 1)
        def _():
            send(src, dst, self.xs.at[i, h], self.wr.at[x, h], wide=ysrc * NZ + z)

        @pl.when(d == 2)
        def _():
            send(src, self.relay_bufs[h], self.xs.at[i, h], self.rr.at[h], wide=rem(x + step, NX) * NZ + z)

    def relay(self, h):
        at = self.at
        x, z, c = at["x"], at["z"], at["c"]
        step = 1 if h == 0 else NX - 1
        k = rem(x + NX - step, NX)
        buf = self.relay_bufs[h]
        wait(buf, self.rr.at[h])
        send(buf, self.spot(k, c, h), self.rs.at[h], self.wr.at[k, h], wide=rem(x + step, NX) * NZ + z)

    def cex(self, dk, h):
        at = self.at
        k = rem(at["x"] + dk + NX, NX)
        ref = self.spot(k, at["c"], h)
        wait(ref, self.wr.at[k, h])
        send(ref, ref, self.ps.at[k, h], self.pr.at[k, h], narrow=2 * at["y"] + 1 - at["c"])

    def cex_all(self):
        for dk, h in ((0, 0), (0, 1), (-1, 0), (1, 1), (-1, 1), (1, 0), (2, 0), (2, 1)):
            self.cex(dk, h)

    def finish(self):
        for k in range(NX):
            for h in range(2):
                wait(self.spot(k, 1 - self.at["c"], h), self.pr.at[k, h])

    def wait_sends(self):
        at = self.at
        ref = self.wy.at[0, self.hs(0), :]
        for i in range(6):
            wait(ref, self.ys.at[i])
        for i in range(NY):
            d = rem(self.yslot(i) - at["x"] + NX, NX)
            for h in range(2):

                @pl.when(d != 0)
                def _():
                    wait(ref, self.xs.at[i, h])

        for h in range(2):
            wait(ref, self.rs.at[h])
        for k in range(NX):
            for h in range(2):
                wait(ref, self.ps.at[k, h])


MOVER_PARTS = 13


def mover_scratch(rows, width):
    dma = pltpu.SemaphoreType.DMA
    return [
        pltpu.VMEM((NY, rows, width), BF16),
        pltpu.VMEM((NX, rows, 2 * width), BF16),
        pltpu.VMEM((rows // 2, width), BF16),
        pltpu.VMEM((rows // 2, width), BF16),
        dma((NY, 2)),
        dma((NX, 2)),
        dma((NX, 2)),
        dma((2,)),
        dma((6,)),
        dma((NY, 2)),
        dma((NX, 2)),
        dma((2,)),
        dma((2,)),
    ]


def as_columns(v):
    size = v.shape[1]
    lane = lax.broadcasted_iota(jnp.int32, (size, size), 0)
    eye = jnp.where(lane == lax.broadcasted_iota(jnp.int32, (size, size), 1), 1.0, 0.0).astype(BF16)
    return lax.dot_general(eye, v, (((1,), (1,)), ((), ())), preferred_element_type=F32)


def project(entries, w1_ref, b1_ref, w2_ref, p_ref, gain_ref, bias_ref, b2_ref, v_ref, *scratch):
    m0s, m1s, m2s = (scratch[i * MOVER_PARTS : (i + 1) * MOVER_PARTS] for i in range(3))
    (wf, cols, b2, gb, gbr, gbs, moments, xn, xf, sx, sz, sxr, sxs, szr, szs, xg, xgr, xgs, xt, part, rz, rzr, rzs, act, ar, asem, ob, orx, orr, ors, vst, vr, vsend) = scratch[3 * MOVER_PARTS :]
    wide, n = lax.axis_index("wide"), lax.axis_index("narrow")
    x, z = wide // NZ, rem(wide, NZ)
    y, c = n // 2, rem(n, 2)
    at = {"x": x, "y": y, "z": z, "c": c, "n": n}
    feats = p_ref.shape[0]
    krows = 4 * feats
    rows = xg.shape[2]
    outs = w2_ref.shape[0]
    block = rows // NZ
    width = m0s[0].shape[2]

    def xdev(d):
        return rem(x + d, NX) * NZ + z

    def zdev(d):
        return x * NZ + rem(z + d, NZ)

    barrier = pltpu.get_barrier_semaphore()
    for d in range(1, NX):
        pl.semaphore_signal(barrier, inc=1, device_id={"wide": xdev(d)}, device_id_type=MESH)
    for d in range(1, NZ):
        pl.semaphore_signal(barrier, inc=1, device_id={"wide": zdev(d)}, device_id_type=MESH)
    for d in (1, 2, 2 * NY - 2, 2 * NY - 1):
        pl.semaphore_signal(barrier, inc=1, device_id={"narrow": rem(n + d, 2 * NY)}, device_id_type=MESH)

    movers = [Mover(at, *m) for m in (m0s, m1s, m2s)]
    first, later, second = movers
    for s in range(4):
        wf[s * feats : (s + 1) * feats, :] = w1_ref[s].astype(F32)
    tail = lax.broadcasted_iota(jnp.int32, (16, 2 * width), 0)
    wf[krows : krows + 16, :] = jnp.where(tail == 0, b1_ref[...].astype(F32), 0.0)
    for g, m in enumerate((first, later)):
        m.wy[y] = wf[:, g * width : (g + 1) * width].astype(BF16)
    pl.semaphore_wait(barrier, NX - 1 + NZ - 1 + 4)

    first.start_y()
    for h in range(2):
        first.xf(0, h)
    second.load([(w2_ref.at[:, pl.ds(g * width, width)], g * outs, outs) for g in range(2)])

    lane = lax.broadcasted_iota(jnp.int32, (512, 512), 0)
    goal = (lane // 32 % 2 * 2 + lane % 2) * 128 + lane // 64 * 16 + lane % 32 // 2
    perm = jnp.where(goal == lax.broadcasted_iota(jnp.int32, (512, 512), 1), 1.0, 0.0).astype(BF16)
    for g in range(p_ref.shape[1] // 512):
        moved = jnp.dot(p_ref[:, g * 512 : (g + 1) * 512], perm, preferred_element_type=F32)
        for s in range(4):
            xf[s * feats : (s + 1) * feats, g * 128 : (g + 1) * 128] = moved[:, s * 128 : (s + 1) * 128]

    def xhalf(k, h):
        return xg.at[k, :, pl.ds(h * (rows // 2), rows // 2)]

    def xsend(i, k, h, d):
        send(xhalf(k, h), xhalf(k, h), xgs.at[i], xgr.at[k, h], wide=xdev(d))

    def xwait(d, h):
        k = rem(x + d, NX)
        wait(xhalf(k, h), xgr.at[k, h])

    xg[x] = xf[...].astype(BF16)
    gb[x, 0] = gain_ref[...]
    gb[x, 1] = bias_ref[...]
    for d in range(1, NX):
        send(gb.at[x], gb.at[x], gbs.at[d], gbr.at[x], wide=xdev(d))
    xsend(0, x, 0, 1)
    xsend(1, x, 1, NX - 1)
    xsend(2, x, 1, 1)
    xsend(3, x, 0, NX - 1)

    def gather_sums(i, carry):
        v = xf[pl.ds(pl.multiple_of(i * 8, 8), 8), :]
        return carry[0] + v, carry[1] + v * v

    zero = jnp.zeros((8, rows), F32)
    sums = lax.fori_loop(0, krows // 8, gather_sums, (zero, zero))
    sx[x, 0:1, :] = jnp.sum(sums[0], axis=0, keepdims=True)
    sx[x, 1:2, :] = jnp.sum(sums[1], axis=0, keepdims=True)
    for d in range(1, NX):
        send(sx.at[x], sx.at[x], sxs.at[d], sxr.at[x], wide=xdev(d))
    b2[...] = as_columns(jnp.broadcast_to(b2_ref[...].astype(F32), (16, outs)).astype(BF16))[:, 0:1]
    first.fwd_y()
    first.xf(-1, 0)
    first.xf(1, 1)
    for d in range(1, NX):
        k = rem(x + d, NX)
        wait(sx.at[k], sxr.at[k])
    sz[z] = (sx[0] + sx[1]) + (sx[2] + sx[3])
    for d in range(1, NZ):
        send(sz.at[z], sz.at[z], szs.at[d], szr.at[z], wide=zdev(d))
    first.wait_y(-1, 1)
    first.xf(-1, 1)
    first.wait_y(1, 0)
    first.xf(1, 0)
    later.start_y()
    for d in range(1, NZ):
        k = rem(z + d, NZ)
        wait(sz.at[k], szr.at[k])
    total = sz[0]
    for k in range(1, NZ):
        total = total + sz[k]
    mean = total[0:1, :] / entries
    moments[0:1, :] = mean
    moments[1:2, :] = lax.rsqrt(total[1:2, :] / entries - mean * mean + 1e-05)

    def normalise(d):
        k = rem(x + d, NX)
        gains, shifts = as_columns(gb[k, 0]), as_columns(gb[k, 1])
        for s in range(4):
            cols[s * feats : (s + 1) * feats, 0:1] = gains[:, s : s + 1]
            cols[s * feats : (s + 1) * feats, 1:2] = shifts[:, s : s + 1]

        def step(i, carry):
            at_rows = pl.ds(pl.multiple_of(i * 16, 16), 16)
            v = xg[k, at_rows, :].astype(F32)
            v = (v - moments[0:1, :]) * moments[1:2, :] * cols[at_rows, 0:1] + cols[at_rows, 1:2]
            xn[k, at_rows, :] = v.astype(BF16)
            return carry

        lax.fori_loop(0, krows // 16, step, 0)

    normalise(0)
    for h in range(2):
        first.wait_y(2, h)
        first.xf(2, h)
    first.relay(0)
    first.relay(1)
    xwait(NX - 1, 0)
    xsend(4, rem(x + NX - 1, NX), 0, 1)
    xwait(1, 1)
    xsend(5, rem(x + 1, NX), 1, NX - 1)
    for d in range(1, NX):
        k = rem(x + d, NX)
        wait(gb.at[k], gbr.at[k])
    later.fwd_y()
    second.start_y()
    xwait(NX - 1, 1)
    normalise(NX - 1)
    xwait(1, 0)
    normalise(1)
    first.cex_all()
    for h in range(2):
        later.xf(0, h)
    later.xf(-1, 0)
    later.xf(1, 1)
    later.wait_y(-1, 1)
    later.xf(-1, 1)
    later.wait_y(1, 0)
    later.xf(1, 0)
    for h in range(2):
        later.wait_y(2, h)
        later.xf(2, h)
    second.fwd_y()
    xwait(2, 0)
    xwait(2, 1)
    normalise(2)
    first.finish()
    for g in range(2):
        for way in range(2):
            for h in range(2):
                rz[g, way, 0 if h == way else 1, h] = jnp.zeros(rz.shape[4:], BF16)

    def block_of(b):
        return pl.ds(pl.multiple_of(b * block, block), block)

    def ends_at(s):
        return rem(z + NZ // 2 - s, NZ), rem(z + NZ // 2 + s, NZ)

    def multiply(g, s):
        ba, bb = ends_at(s)
        bb = jnp.where(s == 0, z, bb)
        for k in range(NX):
            pair = jnp.concatenate([xn[k, :, block_of(ba)], xn[k, :, block_of(bb)]], axis=1)
            xt[:, k * krows : (k + 1) * krows] = pair.T
        left = xt[...]
        weight = movers[g].wg

        def tile(j, carry):
            at_cols = pl.ds(pl.multiple_of(j * width, 128), width)
            right = weight[:, 0:krows, at_cols].reshape(NX * krows, width)
            out = jnp.dot(left, right, preferred_element_type=F32)
            part[g, ba, :, at_cols] = out[:block]
            part[g, bb, :, at_cols] = out[block:]
            return carry

        lax.fori_loop(0, 2, tile, 0)

    mid = block // 2

    def reduce_step(g, s):
        for h, way in ((0, 0), (1, 1), (1, 0), (0, 1)):
            begin = 0 if h == way else 1

            @pl.when(s >= begin)
            def _():
                here = rz.at[g, way, s, h]

                @pl.when(s > begin)
                def _():
                    wait(here, rzr.at[g, way, s, h])

                own = part[g, ends_at(s)[way], h * mid : (h + 1) * mid, :]
                rz[g, way, s, h] = (rz[g, way, s, h].astype(F32) + own).astype(BF16)
                send(here, rz.at[g, way, s + 1, h], rzs.at[g, way, s, h], rzr.at[g, way, s + 1, h], wide=zdev(NZ - 1 if way else 1))

    def act_half(g, b, h):
        return act.at[g, b, pl.ds(h * mid, mid), :]

    def act_send(g, s, b, h, up):
        ref = act_half(g, b, h)
        send(ref, ref, asem.at[g, 0 if up else 1, s, h], ar.at[g, b, h], wide=zdev(1 if up else NZ - 1))

    def await_act(g, b, h):
        wait(act_half(g, b, h), ar.at[g, b, h])

    half_root = 0.7071067811865476

    def activate(g):
        shift = movers[g].wg[0, krows : krows + 16, :].astype(F32)[0:1, :]
        for h in range(2):
            at_rows = slice(h * mid, (h + 1) * mid)
            v = part[g, z, at_rows, :] + shift
            for way in range(2):
                wait(rz.at[g, way, NZ // 2, h], rzr.at[g, way, NZ // 2, h])
                v = v + rz[g, way, NZ // 2, h].astype(F32)
            act[g, z, at_rows, :] = (0.5 * v * (1.0 + lax.erf(v * half_root))).astype(BF16)
            act_send(g, 0, z, h, h == 0)
            act_send(g, 0, z, h, h == 1)

    def blocks_at(s):
        return rem(z - s + NZ, NZ), jnp.where(s == NZ // 2, z, rem(z + s, NZ))

    def pass_on(g, s):
        ba, bb = blocks_at(s)
        await_act(g, ba, 0)

        @pl.when(s < NZ // 2)
        def _():
            act_send(g, s, ba, 0, True)
            await_act(g, bb, 1)
            act_send(g, s, bb, 1, False)

        await_act(g, ba, 1)

        @pl.when(s < NZ // 2 - 1)
        def _():
            act_send(g, s, ba, 1, True)

        @pl.when(s < NZ // 2)
        def _():
            await_act(g, bb, 0)

        @pl.when(s < NZ // 2 - 1)
        def _():
            act_send(g, s, bb, 0, False)

    def front(s, carry):
        multiply(0, s)
        reduce_step(0, s)
        return carry

    lax.fori_loop(0, 2, front, 0)
    later.relay(0)
    later.relay(1)
    for h in range(2):
        second.xf(0, h)
    second.xf(-1, 0)
    second.xf(1, 1)
    lax.fori_loop(2, NZ // 2, front, 0)
    second.wait_y(-1, 1)
    second.xf(-1, 1)
    second.wait_y(1, 0)
    second.xf(1, 0)
    for h in range(2):
        second.wait_y(2, h)
        second.xf(2, h)
    activate(0)
    later.cex_all()
    later.finish()

    def both(s, carry):
        multiply(1, s)
        reduce_step(1, s)
        pass_on(0, s + 1)
        return carry

    lax.fori_loop(0, 2, both, 0)
    second.relay(0)
    second.relay(1)
    lax.fori_loop(2, NZ // 2, both, 0)
    activate(1)
    second.cex_all()
    second.finish()
    w2g = second.wg

    def gather_step(s):
        pass_on(1, s)
        ba, bb = blocks_at(s)
        left = [jnp.concatenate([act[g, ba], act[g, bb]], axis=0) for g in range(2)]

        def out_block(k, carry):
            out = 0.0
            for g in range(2):
                right = w2g[k, g * outs : (g + 1) * outs, :]
                out = out + lax.dot_general(right, left[g], (((1,), (1,)), ((), ())), preferred_element_type=F32)
            ob[s - 1, k] = out.astype(BF16)
            return carry

        lax.fori_loop(0, NX, out_block, 0)
        for d in range(1, NX):
            k = rem(x + d, NX)
            send(ob.at[s - 1, k], orx.at[s - 1, x], ors.at[s - 1, d], orr.at[s - 1, x], wide=xdev(d))

    def outgoing(d, t):
        q = n + d
        slot = t - 5 * q + 8
        ok = (q >= 0) & (q < 2 * NY) & (slot >= 0) & (slot < SLOTS)
        return q, slot, ok

    def finish_step(s):
        for d in range(1, NX):
            k = rem(x + d, NX)
            wait(orx.at[s - 1, k], orr.at[s - 1, k])
        value = ob[s - 1, x].astype(F32) + b2[...]
        for d in range(1, NX):
            value = value + orx[s - 1, rem(x + d, NX)].astype(F32)
        value = value.astype(BF16)
        for i, b in enumerate(blocks_at(s)):
            vst[s - 1, i] = value[:, i * block : (i + 1) * block]
            src = vst.at[s - 1, i]
            t = 4 * n + b // 2
            own = 2 * (t - 5 * n + 8) + rem(b, 2)
            pltpu.make_async_copy(src, v_ref.at[own], vr.at[own]).start()
            for j, d in enumerate((-2, -1, 1, 2)):
                q, slot, ok = outgoing(d, t)

                @pl.when(ok)
                def _():
                    there = 2 * slot + rem(b, 2)
                    send(src, v_ref.at[there], vsend.at[s - 1, i, j], vr.at[there], narrow=q)

    def last(s, carry):
        gather_step(s)

        @pl.when(s > 1)
        def _():
            finish_step(s - 1)

        return carry

    lax.fori_loop(1, NZ // 2 + 1, last, 0)
    finish_step(NZ // 2)

    for there in range(2 * SLOTS):
        t = 5 * n - 8 + there // 2

        @pl.when((t >= 0) & (t < 8 * NY))
        def _():
            wait(vst.at[0, 0], vr.at[there])

    for s in range(1, NZ // 2 + 1):
        for i, b in enumerate(blocks_at(s)):
            t = 4 * n + b // 2
            for j, d in enumerate((-2, -1, 1, 2)):
                ok = outgoing(d, t)[2]

                @pl.when(ok)
                def _():
                    wait(vst.at[0, 0], vsend.at[s - 1, i, j])

        for d in range(1, NX):
            wait(ob.at[0, 0], ors.at[s - 1, d])
    for g in range(2):
        for s in range(NZ // 2):
            for h in range(2):
                for up in range(2):
                    if s < NZ // 2 - 1 or h == up:
                        wait(act_half(0, 0, 0), asem.at[g, up, s, h])
        for s in range(NZ // 2):
            for h in range(2):
                for way in range(2):
                    if s > 0 or h == way:
                        wait(rz.at[0, 0, 0, 0], rzs.at[g, way, s, h])
    for d in range(1, NX):
        wait(sx.at[0], sxs.at[d])
        wait(gb.at[0], gbs.at[d])
    for d in range(1, NZ):
        wait(sz.at[0], szs.at[d])
    for i in range(6):
        wait(xhalf(0, 0), xgs.at[i])
    for m in movers:
        m.wait_sends()


def place(pos_ref, v_ref, text_ref, out_ref, acc, covered):
    n = lax.axis_index("narrow")
    cols = text_ref.shape[1]
    acc[...] = jnp.zeros_like(acc)
    covered[...] = jnp.zeros_like(covered)

    def step(slot, carry):
        t = 5 * n - 8 + slot
        valid = (t >= 0) & (t < 8 * NY)
        start = pos_ref[jnp.clip(t, 0, 8 * NY - 1) * TILE_ROWS] - n * cols

        @pl.when(valid & (start > -TILE_ROWS) & (start < cols))
        def _():
            row = lax.broadcasted_iota(jnp.int32, (TILE_ROWS, cols), 0)
            col = lax.broadcasted_iota(jnp.int32, (TILE_ROWS, cols), 1)
            hot = jnp.where(row + start == col, 1.0, 0.0).astype(BF16)
            tile = jnp.concatenate([v_ref[2 * slot], v_ref[2 * slot + 1]], axis=1)
            acc[...] += jnp.dot(tile, hot, preferred_element_type=F32)
            at_col = lax.broadcasted_iota(jnp.int32, covered.shape, 1)
            inside = (at_col >= start) & (at_col < start + TILE_ROWS)
            covered[...] = jnp.where(inside, 1.0, covered[...])

        return carry

    lax.fori_loop(0, SLOTS, step, 0)
    out_ref[...] = jnp.where(covered[0:1, :] > 0, acc[...].astype(BF16), text_ref[...])


def shards(patches, ln_gain, ln_bias, first_weight, first_bias, second_weight, second_bias, text_embeds, vis_pos):
    feats = patches.shape[0]
    krows = 4 * feats
    rows = patches.shape[1] // 4
    width = first_weight.shape[2] // 2
    outs = second_weight.shape[0]
    block = rows // NZ
    dma = pltpu.SemaphoreType.DMA
    vmem = pl.BlockSpec(memory_space=pltpu.VMEM)
    scratch = (
        mover_scratch(krows + 16, width)
        + mover_scratch(krows + 16, width)
        + mover_scratch(2 * outs, width)
        + [
            pltpu.VMEM((krows + 16, 2 * width), F32),
            pltpu.VMEM((krows, 2), F32),
            pltpu.VMEM((outs, 1), F32),
            pltpu.VMEM((NX, 2, 4, feats), BF16),
            dma((NX,)),
            dma((NX,)),
            pltpu.VMEM((2, rows), F32),
            pltpu.VMEM((NX, krows, rows), BF16),
            pltpu.VMEM((krows, rows), F32),
            pltpu.VMEM((NX, 2, rows), F32),
            pltpu.VMEM((NZ, 2, rows), F32),
            dma((NX,)),
            dma((NX,)),
            dma((NZ,)),
            dma((NZ,)),
            pltpu.VMEM((NX, krows, rows), BF16),
            dma((NX, 2)),
            dma((6,)),
            pltpu.VMEM((2 * block, NX * krows), BF16),
            pltpu.VMEM((2, NZ, block, 2 * width), F32),
            pltpu.VMEM((2, 2, NZ // 2 + 1, 2, block // 2, 2 * width), BF16),
            dma((2, 2, NZ // 2 + 1, 2)),
            dma((2, 2, NZ // 2, 2)),
            pltpu.VMEM((2, NZ, block, 2 * width), BF16),
            dma((2, NZ, 2)),
            dma((2, 2, NZ // 2, 2)),
            pltpu.VMEM((NZ // 2, NX, outs, 2 * block), BF16),
            pltpu.VMEM((NZ // 2, NX, outs, 2 * block), BF16),
            dma((NZ // 2, NX)),
            dma((NZ // 2, NX)),
            pltpu.VMEM((NZ // 2, 2, outs, block), BF16),
            dma((2 * SLOTS,)),
            dma((NZ // 2, 2, 4)),
        ]
    )
    moved = pl.pallas_call(
        functools.partial(project, float(4 * feats * NX * NZ)),
        out_shape=jax.ShapeDtypeStruct((2 * SLOTS, outs, block), BF16),
        in_specs=[vmem] * 7,
        out_specs=pl.BlockSpec(memory_space=pl.ANY),
        scratch_shapes=scratch,
        compiler_params=pltpu.CompilerParams(
            collective_id=0, has_side_effects=True, vmem_limit_bytes=63 * 1024 * 1024
        ),
        name="project",
    )(first_weight, first_bias[None, :], second_weight, patches, ln_gain, ln_bias, second_bias[None, :])
    return pl.pallas_call(
        place,
        out_shape=jax.ShapeDtypeStruct(text_embeds.shape, BF16),
        in_specs=[pl.BlockSpec(memory_space=pltpu.SMEM), vmem, vmem],
        out_specs=vmem,
        scratch_shapes=[pltpu.VMEM(text_embeds.shape, F32), pltpu.VMEM((8, text_embeds.shape[1]), F32)],
        name="place",
    )(vis_pos, moved, text_embeds)


def solution(mesh):
    in_specs = (
        P("wide", "narrow"),
        P(None, "wide"),
        P(None, "wide"),
        P(None, "wide", "narrow"),
        P("narrow"),
        P("wide", "narrow"),
        P("wide"),
        P("wide", "narrow"),
        P(),
    )
    out_specs = P("wide", "narrow")
    return jax.shard_map(shards, mesh=mesh, in_specs=in_specs, out_specs=out_specs, check_vma=False)
```
